32 devices in a mesh: dp: 8 (over y, x, core), head: 4 (over z).
Axes of the slice: x: 2, y: 2, z: 4, core: 2. Of those that a mesh axis runs over, the one named last changes fastest.
Arguments:
- acts: bfloat16 [8, 128, 4096], P('dp', None, 'head'), may hold values from -6 to 6
- grads: bfloat16 [8, 128, 4096], P('dp', None, 'head'), may hold values from -0.5390625 to 0.5390625
- query_acts: bfloat16 [512, 4096], P('dp', 'head'), may hold values from -6 to 6
- query_grads: bfloat16 [512, 4096], P('dp', 'head'), may hold values from -0.26953125 to 0.26953125
- basis_in: bfloat16 [4096, 4096], P('dp'), may hold values from -0.09375 to 0.09375
- basis_out: bfloat16 [4096, 4096], P('dp'), may hold values from -0.09375 to 0.09375
- damping: float32 [1], replicated, may hold values from 0.1 to 1
Outputs:
- update: bfloat16 [4096, 4096], P('dp', 'head')
- corrections: float32 [4096, 4096], P('dp', 'head')
- scores: float32 [8], replicated
The draws below stay inside these ranges and needn't reach their ends.
All inputs are finite; a program needn't handle non-finite values.
Results may differ from the reference program's by a relative error of at most 0.0056.
Values may be sent and summed in bfloat16 or wider, within the bound.
A program may use at most 128 MiB of HBM per device.

```python
import math
import jax
import jax.numpy as jnp
from jax import lax

DIN = 4096
DOUT = 4096
TLEN = 128
QLEN = 512
SEQS = 8


def shard_levels(stream_key, dims, cuts, low, high):
    loudness, own = 1.0, jax.random.fold_in(stream_key, 6)
    for dim, parts in cuts:
        draws = jnp.exp(jax.random.uniform(jax.random.fold_in(own, dim), (parts,), jnp.float32, low / len(cuts), high / len(cuts)))
        loudness = loudness * jnp.repeat(draws, dims[dim] // parts).reshape([-1 if axis == dim else 1 for axis in range(len(dims))])
    return loudness


def gaussian(key, shape, scale, bound, split=(), kind=jnp.bfloat16):
    values = scale * jax.random.normal(key, shape, jnp.float32)
    if split:
        values = values * shard_levels(key, shape, split, -0.22, 0.18)
    return jnp.clip(values, -bound, bound).astype(kind)


def setup_inputs(seed: int = 0) -> dict:
    streams_of = jax.random.split(jax.random.key(seed), 8)
    return {
        "acts": gaussian(streams_of[0], (SEQS, TLEN, DIN), 1.0, 6.0, ((0, 8), (2, 4))),
        "grads": gaussian(streams_of[1], (SEQS, TLEN, DOUT), 0.09, 0.5390625, ((0, 8), (2, 4))),
        "query_acts": gaussian(streams_of[2], (QLEN, DIN), 1.0, 6.0, ((0, 8), (1, 4))),
        "query_grads": gaussian(streams_of[3], (QLEN, DOUT), 0.045, 0.26953125, ((0, 8), (1, 4))),
        "basis_in": gaussian(streams_of[4], (DIN, DIN), DIN ** -0.5, 0.09375, ((0, 8),)),
        "basis_out": gaussian(streams_of[5], (DOUT, DOUT), DOUT ** -0.5, 0.09375, ((0, 8),)),
        "damping": jnp.clip(jnp.exp(jax.random.uniform(streams_of[6], (1,), jnp.float32, math.log(0.1), math.log(1.0))), 0.1, 1.0),
    }


def contract_rows(left_rows, right_rows):
    return lax.dot_general(left_rows, right_rows, (((0,), (0,)), ((), ())), preferred_element_type=jnp.float32)

def reference(acts, grads, query_acts, query_grads, basis_in, basis_out, damping):
    rot_in = jnp.dot(acts.reshape(SEQS * TLEN, DIN), basis_in, preferred_element_type=jnp.float32).astype(jnp.bfloat16)
    rot_out = jnp.dot(grads.reshape(SEQS * TLEN, DOUT), basis_out, preferred_element_type=jnp.float32).astype(jnp.bfloat16)
    query_in = jnp.dot(query_acts, basis_in, preferred_element_type=jnp.float32).astype(jnp.bfloat16)
    query_out = jnp.dot(query_grads, basis_out, preferred_element_type=jnp.float32).astype(jnp.bfloat16)

    def accumulate(running, seq_index):
        offset = (seq_index * TLEN).astype(jnp.int32)
        out_seq = lax.dynamic_slice_in_dim(rot_out, offset, TLEN, 0)
        in_seq = lax.dynamic_slice_in_dim(rot_in, offset, TLEN, 0)
        per_seq = contract_rows(out_seq, in_seq)
        return (running + per_seq * per_seq, None)
    summed, ignored = lax.scan(accumulate, jnp.zeros((DOUT, DIN), jnp.float32), jnp.arange(SEQS, dtype=jnp.int32))
    corrections = summed / SEQS
    rotated_query = contract_rows(query_out, query_in)
    scaled = (rotated_query / (corrections + damping[0])).astype(jnp.bfloat16)
    mapped = jnp.dot(rot_in, scaled.T, preferred_element_type=jnp.float32)
    products = rot_out.astype(jnp.float32) * mapped
    scores = lax.optimization_barrier(jnp.sum(products.reshape(SEQS, TLEN * DOUT), axis=1)) / math.sqrt(DIN * DOUT)
    back = jnp.dot(scaled, basis_in.T, preferred_element_type=jnp.float32).astype(jnp.bfloat16)
    update = jnp.dot(basis_out, back, preferred_element_type=jnp.float32).astype(jnp.bfloat16)
    return (update, corrections, scores)
```

```python
import functools
import math

import jax
import jax.numpy as jnp
from jax import lax
from jax.experimental import pallas as pl
from jax.experimental.pallas import tpu as pltpu
from jax.sharding import PartitionSpec as P

MESH = pl.DeviceIdType.MESH
ANY = pl.BlockSpec(memory_space=pl.ANY)
IN_VMEM = pl.BlockSpec(memory_space=pltpu.VMEM)
IN_SMEM = pl.BlockSpec(memory_space=pltpu.SMEM)
cores = 2
most_columns = 256
halves = 2


class Place:
    def __init__(self):
        self.data_size = lax.axis_size("dp")
        self.head_size = lax.axis_size("head")
        self.chips = self.data_size // cores
        self.column_count = 2 if self.chips % 2 == 0 else 1
        self.row_count = self.chips // self.column_count
        self.data = lax.axis_index("dp")
        self.head = lax.axis_index("head")
        self.core = lax.rem(self.data, cores)
        self.chip = self.data // cores
        self.row = self.chip // self.column_count
        self.column = lax.rem(self.chip, self.column_count)

    def at(self, down=0, right=0, flip=False):
        row = lax.rem(self.row + down + self.row_count, self.row_count)
        column = lax.rem(self.column + right + self.column_count, self.column_count)
        core = (cores - 1) - self.core if flip else self.core
        return (row * self.column_count + column) * cores + core

    def enter(self):
        barrier = pltpu.get_barrier_semaphore()
        for step in range(1, self.data_size):
            other = lax.rem(self.data + step, self.data_size)
            pl.semaphore_signal(
                barrier, inc=1, device_id={"dp": other, "head": self.head}, device_id_type=MESH
            )
        for step in range(1, self.head_size):
            other = lax.rem(self.head + step, self.head_size)
            pl.semaphore_signal(
                barrier, inc=1, device_id={"dp": self.data, "head": other}, device_id_type=MESH
            )
        pl.semaphore_wait(barrier, self.data_size + self.head_size - 2)


class Copies:
    def __init__(self, place, send_sems, recv_sems, local_sems=None):
        self.place, self.send_sems, self.recv_sems = place, send_sems, recv_sems
        self.local_sems, self.used, self.local_used = local_sems, 0, 0
        self.to_drain = []

    def slot(self):
        self.used += 1
        return self.used - 1

    def make(self, slot, src, dst, data=None, head=None):
        place = self.place
        return pltpu.make_async_remote_copy(
            src_ref=src,
            dst_ref=dst,
            send_sem=self.send_sems.at[slot],
            recv_sem=self.recv_sems.at[slot],
            device_id={
                "dp": place.data if data is None else data,
                "head": place.head if head is None else head,
            },
            device_id_type=MESH,
        )

    def send(self, src, dst, data=None, head=None):
        copy = self.make(self.slot(), src, dst, data, head)
        copy.start()
        self.to_drain.append(copy.wait_send)
        return copy

    def local(self, src, dst):
        copy = pltpu.make_async_copy(src, dst, self.local_sems.at[self.local_used])
        self.local_used += 1
        copy.start()
        return copy

    def drain(self):
        for wait in self.to_drain:
            wait()


class PlaneGather:
    def __init__(self, copies, own, slot, rows):
        self.copies, self.own, self.slot, self.rows = copies, own, slot, rows
        low = max(rows // 2 // 16 * 16, 1)
        self.low, self.high = (0, low), (low, rows - low)

    def first(self):
        c, place = self.copies, self.copies.place
        self.right, self.down = {}, {}
        for right_half, down_half in ((self.low, self.high), (self.high, self.low)):
            for right in range(1, place.column_count):
                self.right[right, right_half] = c.send(
                    self.own(*right_half),
                    self.slot(place.data, *right_half),
                    place.at(right=right),
                )
            for down in range(1, place.row_count):
                self.down[down, down_half] = c.send(
                    self.own(*down_half), self.slot(place.data, *down_half), place.at(down=down)
                )
        whole = (0, self.rows)
        self.flips = [
            c.send(self.own(*whole), self.slot(place.data, *whole), place.at(flip=True))
        ]

    def flip(self, index):
        place = self.copies.place
        block = self.slot(index, 0, self.rows)
        self.flips.append(self.copies.send(block, block, place.at(flip=True)))

    def second(self):
        c, place = self.copies, self.copies.place
        self.corner = {}
        for right in range(1, place.column_count):
            self.right[right, self.low].wait_recv()
            block = self.slot(place.at(right=-right), *self.low)
            for down in range(1, place.row_count):
                self.corner[down, right, 0] = c.send(block, block, place.at(down=down))
        for down in range(1, place.row_count):
            self.down[down, self.high].wait_recv()
            block = self.slot(place.at(down=-down), *self.high)
            for right in range(1, place.column_count):
                self.corner[down, right, 1] = c.send(block, block, place.at(right=right))

    def third(self):
        place = self.copies.place
        for right in range(1, place.column_count):
            self.right[right, self.high].wait_recv()
            self.flip(place.at(right=-right))
        for down in range(1, place.row_count):
            self.down[down, self.low].wait_recv()
            self.flip(place.at(down=-down))

    def fourth(self):
        place = self.copies.place
        for down in range(1, place.row_count):
            for right in range(1, place.column_count):
                self.corner[down, right, 0].wait_recv()
                self.corner[down, right, 1].wait_recv()
                self.flip(place.at(down=-down, right=-right))

    def last(self):
        for copy in self.flips:
            copy.wait_recv()


class LineGather:
    def __init__(self, copies, own, slot):
        self.copies, self.own, self.slot = copies, own, slot
        steps = range(1, copies.place.head_size)
        self.up = {step: copies.slot() for step in steps}
        self.down = {step: copies.slot() for step in steps}

    def hand_on(self, step):
        place = self.copies.place
        head, size = place.head, place.head_size
        for slots, sign in ((self.up, 1), (self.down, -1)):
            owner = head - sign * (step - 1)
            inside = (head + sign >= 0) & (head + sign < size) & (owner >= 0) & (owner < size)

            def copy(slots=slots, sign=sign, owner=owner):
                src = self.own if step == 1 else self.slot(owner)
                return self.copies.make(
                    slots[step], src, self.slot(owner), head=head + sign
                )

            pl.when(inside)(lambda copy=copy: copy().start())

            def drain(copy=copy, inside=inside):
                pl.when(inside)(lambda: copy().wait_send())

            self.copies.to_drain.append(drain)

    def arrive(self, step):
        place = self.copies.place
        head, size = place.head, place.head_size
        for slots, sign in ((self.up, 1), (self.down, -1)):
            owner = head - sign * step

            def wait(slots=slots, owner=owner):
                block = self.slot(owner)
                self.copies.make(slots[step], block, block, head=head).wait_recv()

            pl.when((owner >= 0) & (owner < size))(wait)


def gather_inputs_kernel(
    acts, grads, basis_in, basis_out, columns, acts_full, grads_wide, grads_chip, basis_pair,
    held_columns, held_acts, held_grads, send_sems, recv_sems, local_sems,
):
    place = Place()
    c = Copies(place, send_sems, recv_sems, local_sems)
    head, size = place.head, place.head_size
    width = acts.shape[1]
    rows, block = columns.shape[1], basis_pair.shape[2]
    chip_width = grads_chip.shape[2]
    span = pl.ds(pl.multiple_of(head * width, width), width)
    place.enter()
    wide = []
    for step in range(1, size):
        other = lax.rem(head + step, size)
        wide.append(c.send(grads.at[other], grads_wide.at[:, span], head=other))
    line = LineGather(
        c,
        acts,
        lambda owner: acts_full.at[:, pl.ds(pl.multiple_of(owner * width, width), width)],
    )
    line.hand_on(1)
    plane = PlaneGather(
        c,
        lambda low, count: basis_in.at[pl.ds(low, count), span],
        lambda index, low, count: columns.at[index, pl.ds(low, count), :],
        rows,
    )
    plane.first()
    pairs = []
    for chip in range(place.chips):
        start = pl.multiple_of((chip * cores + (cores - 1) - place.core) * block, block)
        pairs.append(
            c.send(basis_out.at[:, pl.ds(start, block)], basis_pair.at[chip], place.at(flip=True))
        )
    loads = [
        c.local(grads.at[head], held_grads),
        c.local(acts, held_acts),
        c.local(basis_in.at[:, span], held_columns),
    ]
    for load in loads:
        load.wait()
    stores = [
        c.local(held_grads, grads_wide.at[:, span]),
        c.local(held_acts, acts_full.at[:, span]),
        c.local(held_columns, columns.at[place.data]),
    ]
    stores[0].wait()
    for copy in wide:
        copy.wait_recv()

    def chip_span(chip):
        return pl.ds(pl.multiple_of(chip * chip_width, chip_width), chip_width)

    across, flips = [], []
    mine = c.local(grads_wide.at[:, chip_span(place.chip)], grads_chip.at[place.data])
    for step in range(1, place.chips):
        chip = lax.rem(place.chip + step, place.chips)
        across.append(
            c.send(
                grads_wide.at[:, chip_span(chip)],
                grads_chip.at[place.data],
                chip * cores + place.core,
            )
        )
    flips.append(
        c.send(
            grads_wide.at[:, chip_span(place.chip)],
            grads_chip.at[place.data],
            place.at(flip=True),
        )
    )
    for step in range(1, size - 1):
        line.arrive(step)
        line.hand_on(step + 1)
    plane.second()
    for step, copy in zip(range(1, place.chips), across):
        copy.wait_recv()
        source = lax.rem(place.chip - step + place.chips, place.chips) * cores + place.core
        flips.append(c.send(grads_chip.at[source], grads_chip.at[source], place.at(flip=True)))
    plane.third()
    plane.fourth()
    if size > 1:
        line.arrive(size - 1)
    plane.last()
    for copy in pairs + flips:
        copy.wait_recv()
    mine.wait()
    for store in stores[1:]:
        store.wait()
    c.drain()


def scatter_kernel(parts, landed, held, send_sems, recv_sems, local_sems):
    place = Place()
    c = Copies(place, send_sems, recv_sems, local_sems)
    place.enter()
    sent = []
    for step in range(1, place.chips):
        chip = lax.rem(place.chip + step, place.chips)
        sent.append(
            c.send(parts.at[chip], landed.at[place.chip], chip * cores + place.core)
        )
    c.local(parts.at[place.chip], held).wait()
    c.local(held, landed.at[place.chip]).wait()
    for copy in sent:
        copy.wait_recv()
    c.drain()


def gather_rotated_kernel(
    rotated_out, rotated_in, out_all, in_all, held_out, held_in, send_sems, recv_sems, local_sems
):
    place = Place()
    c = Copies(place, send_sems, recv_sems, local_sems)
    place.enter()
    line = LineGather(c, rotated_out, lambda owner: out_all.at[:, owner])
    line.hand_on(1)
    plane = PlaneGather(
        c,
        lambda low, count: rotated_in.at[pl.ds(low, count), :],
        lambda index, low, count: in_all.at[index, pl.ds(low, count), :],
        rotated_in.shape[0],
    )
    plane.first()
    loads = [c.local(rotated_out, held_out), c.local(rotated_in, held_in)]
    for load in loads:
        load.wait()
    stores = [c.local(held_out, out_all.at[:, place.head]), c.local(held_in, in_all.at[place.data])]
    plane.second()
    plane.third()
    for step in range(1, place.head_size):
        line.arrive(step)
        if step + 1 < place.head_size:
            line.hand_on(step + 1)
        if step == 1:
            plane.fourth()
    if place.head_size == 1:
        plane.fourth()
    plane.last()
    for store in stores:
        store.wait()
    c.drain()


def tile_kernel(
    seq_here, seq_len, damping, out_all, in_all, corrections, scaled, scores, products
):
    data_size = out_all.shape[0]
    train_rows = seq_here * seq_len
    seq_count = data_size * seq_here

    def product(left, right):
        return lax.dot_general(
            left, right, (((0,), (0,)), ((), ())), preferred_element_type=jnp.float32
        )

    total = jnp.zeros(corrections.shape, jnp.float32)
    for seq in range(seq_count):
        owner, start = seq // seq_here, (seq % seq_here) * seq_len
        rows = slice(start, start + seq_len)
        value = product(out_all[owner, rows, :], in_all[owner, rows, :])
        products[seq] = value
        total = total + value * value
    mean = total / seq_count
    corrections[...] = mean
    query_out = out_all[:, train_rows:, :].reshape(-1, out_all.shape[2])
    query_in = in_all[:, train_rows:, :].reshape(-1, in_all.shape[2])
    ratio = (product(query_out, query_in) / (mean + damping[0])).astype(jnp.bfloat16)
    scaled[...] = ratio
    weights = ratio.astype(jnp.float32)
    for seq in range(seq_count):
        scores[0, seq, :] = jnp.sum(products[seq] * weights, axis=0)


def finish_kernel(
    scaled, columns, basis, partial_scores, update, scores, held_columns, held_basis, rising,
    falling, back, whole_part, score_line, score_plane, score_sum, line_send, line_recv,
    plane_send, plane_recv, flip_send, flip_recv, score_send, score_recv, local_sems,
):
    place = Place()
    head, size = place.head, place.head_size
    rows, width = scaled.shape
    turns, piece = rising.shape[1], rising.shape[3]
    halves = line_send.shape[3]
    half_rows = rows // halves
    loads = [
        pltpu.make_async_copy(columns, held_columns, local_sems.at[0]),
        pltpu.make_async_copy(basis, held_basis, local_sems.at[1]),
    ]
    for load in loads:
        load.start()
    place.enter()
    c = Copies(place, score_send, score_recv)
    line_sent = []
    for step in range(1, size):
        other = lax.rem(head + step, size)
        line_sent.append(c.send(partial_scores, score_line.at[step], head=other))
    plane_slots = {step: c.slot() for step in range(1, place.data_size)}

    def plane_score(step):
        other = lax.rem(place.data + step, place.data_size)
        return c.make(plane_slots[step], score_sum, score_plane.at[step], other)

    def span(half):
        return pl.ds(half * half_rows, half_rows)

    def product(target, turn):
        start = pl.multiple_of(target * width + turn * piece, piece)
        whole_part[...] = lax.dot_general(
            scaled[...],
            held_columns[pl.ds(start, piece), :],
            (((1,), (1,)), ((), ())),
            preferred_element_type=jnp.float32,
        )

    def message(sign, target, turn, half):
        block = (rising if sign == 1 else falling).at[target, turn, span(half), :]
        way = 0 if sign == 1 else 1
        return pltpu.make_async_remote_copy(
            src_ref=block,
            dst_ref=block,
            send_sem=line_send.at[way, target, turn, half],
            recv_sem=line_recv.at[way, target, turn, half],
            device_id={"dp": place.data, "head": head + sign},
            device_id_type=MESH,
        )

    def each_target(visit):
        def step(index, carry):
            for sign in (1, -1):
                target = size - 1 - index if sign == 1 else index
                ahead = target > head if sign == 1 else target < head
                pl.when(ahead)(lambda sign=sign, target=target: visit(sign, target))
            return carry

        lax.fori_loop(0, size - 1, step, 0)

    def relay(turn):
        def visit(sign, target):
            buffer = rising if sign == 1 else falling
            starts = head == (0 if sign == 1 else size - 1)
            product(target, turn)
            for half in range(halves):
                own = whole_part.at[span(half), :]

                @pl.when(jnp.logical_not(starts))
                def add():
                    message(sign, target, turn, half).wait_recv()
                    own[...] = own[...] + buffer[target, turn, span(half), :].astype(jnp.float32)

                buffer[target, turn, span(half), :] = own[...].astype(buffer.dtype)
                message(sign, target, turn, half).start()

        each_target(visit)

    def plane_copy(step, turn, half):
        block = back.at[turn, place.data, span(half), :]
        chip = lax.rem(place.chip + step, place.chips)
        return pltpu.make_async_remote_copy(
            src_ref=block,
            dst_ref=block,
            send_sem=plane_send.at[step, turn, half],
            recv_sem=plane_recv.at[step, turn, half],
            device_id={"dp": chip * cores + place.core, "head": head},
            device_id_type=MESH,
        )

    def source(step):
        return lax.rem(place.chip - step + place.chips, place.chips) * cores + place.core

    def flip_copy(step, turn, half):
        block = back.at[turn, source(step), span(half), :]
        return pltpu.make_async_remote_copy(
            src_ref=block,
            dst_ref=block,
            send_sem=flip_send.at[step, turn, half],
            recv_sem=flip_recv.at[step, turn, half],
            device_id={"dp": place.at(flip=True), "head": head},
            device_id_type=MESH,
        )

    def finish(turn):
        product(head, turn)
        for half in range(halves):
            own = whole_part.at[span(half), :]
            for sign in (1, -1):
                buffer = rising if sign == 1 else falling

                @pl.when(head > 0 if sign == 1 else head < size - 1)
                def add():
                    message(sign, head, turn, half).wait_recv()
                    own[...] = own[...] + buffer[head, turn, span(half), :].astype(jnp.float32)

            back[turn, place.data, span(half), :] = own[...].astype(back.dtype)
            for step in range(1, place.chips):
                plane_copy(step, turn, half).start()
            flip_copy(0, turn, half).start()

    def forward(turn):
        for half in range(halves):
            for step in range(1, place.chips):
                plane_copy(step, turn, half).wait_recv()
                flip_copy(step, turn, half).start()

    def rotate(turn):
        for half in range(halves):
            for step in range(place.chips):
                flip_copy(step, turn, half).wait_recv()
        start = pl.multiple_of(turn * piece, piece)
        update[:, pl.ds(start, piece)] = jnp.dot(
            held_basis[...],
            back[turn].reshape(place.data_size * rows, piece),
            preferred_element_type=jnp.float32,
        ).astype(update.dtype)

    for load in loads:
        load.wait()

    def turn_of(index, carry):
        pl.when(index < turns)(lambda: relay(index))

        @pl.when(index == 0)
        def gather_scores():
            total = partial_scores[...]
            for step, copy in zip(range(1, size), line_sent):
                copy.wait_recv()
                total = total + score_line[step]
            score_sum[...] = total
            for step in range(1, place.data_size):
                plane_score(step).start()

        for lag, stage in ((1, finish), (2, forward), (3, rotate)):
            ready = jnp.logical_and(index >= lag, index < turns + lag)
            pl.when(ready)(lambda lag=lag, stage=stage: stage(index - lag))
        return carry

    lax.fori_loop(0, turns + 3, turn_of, 0)
    total = score_sum[...]
    for step in range(1, place.data_size):
        plane_score(step).wait_recv()
        total = total + score_plane[step]
    scores[...] = total

    def drain(turn, carry):
        for half in range(halves):
            each_target(lambda sign, target: message(sign, target, turn, half).wait_send())
            for step in range(1, place.chips):
                plane_copy(step, turn, half).wait_send()
            for step in range(place.chips):
                flip_copy(step, turn, half).wait_send()
        return carry

    lax.fori_loop(0, turns, drain, 0)
    for step in range(1, place.data_size):
        plane_score(step).wait_send()
    c.drain()


def sems(remote, local):
    return [
        pltpu.SemaphoreType.DMA((remote,)),
        pltpu.SemaphoreType.DMA((remote,)),
        pltpu.SemaphoreType.DMA((local,)),
    ]


def talking(number):
    return pltpu.CompilerParams(collective_id=number, has_side_effects=True)


def shaped(*shape, dtype=jnp.bfloat16):
    return jax.ShapeDtypeStruct(shape, dtype)


def per_device(acts, grads, query_acts, query_grads, basis_in, basis_out, damping):
    seq_here, seq_len, width = acts.shape
    data_size = lax.axis_size("dp")
    head_size = lax.axis_size("head")
    chips = data_size // cores
    basis_rows, full_in = basis_in.shape
    full_out = basis_out.shape[1]
    block = full_out // data_size
    grads_width = grads.shape[2]
    train_rows = seq_here * seq_len
    acts_rows = jnp.concatenate([acts.reshape(train_rows, width), query_acts], axis=0)
    grads_rows = jnp.concatenate([grads.reshape(train_rows, grads_width), query_grads], axis=0)
    row_count = acts_rows.shape[0]
    share = row_count // head_size
    chip_width = full_out // chips
    bf16 = jnp.bfloat16
    gather_copies = 8 * data_size + 4 * head_size

    columns, acts_full, ignored, grads_chip, basis_pair = pl.pallas_call(
        gather_inputs_kernel,
        out_shape=(
            shaped(data_size, basis_rows, width),
            shaped(row_count, full_in),
            shaped(share, full_out),
            shaped(data_size, share, chip_width),
            shaped(chips, basis_rows, block),
        ),
        in_specs=[ANY] * 4,
        out_specs=(ANY,) * 5,
        scratch_shapes=[
            pltpu.VMEM((basis_rows, width), bf16),
            pltpu.VMEM((row_count, width), bf16),
            pltpu.VMEM((share, grads_width), bf16),
        ]
        + sems(gather_copies, 8),
        compiler_params=talking(0),
        name="gather_inputs",
    )(acts_rows, grads_rows.reshape(head_size, share, grads_width), basis_in, basis_out)
    columns = columns.reshape(full_in, width)

    core = lax.rem(lax.axis_index("dp"), cores)
    grads_pair = grads_chip.reshape(data_size * share, chip_width)
    own_grads = lax.dynamic_slice_in_dim(grads_pair, core * basis_rows, basis_rows, 1)
    pair_grads = lax.dynamic_slice_in_dim(
        grads_pair, ((cores - 1) - core) * basis_rows, basis_rows, 1
    )
    own_parts = [
        jnp.dot(
            own_grads,
            lax.dynamic_slice_in_dim(basis_out, (chip * cores + core) * block, block, 1),
            preferred_element_type=jnp.float32,
        )
        + jnp.dot(pair_grads, basis_pair[chip], preferred_element_type=jnp.float32)
        for chip in range(chips)
    ]
    parts = jnp.stack([part.astype(bf16) for part in own_parts])
    landed = pl.pallas_call(
        scatter_kernel,
        out_shape=shaped(chips, data_size * share, block),
        in_specs=[ANY],
        out_specs=ANY,
        scratch_shapes=[pltpu.VMEM((data_size * share, block), bf16)] + sems(chips, 2),
        compiler_params=talking(1),
        name="scatter_rotated",
    )(parts)
    rotated_out = jnp.sum(landed.astype(jnp.float32), axis=0).astype(bf16)
    rotated_in = jnp.dot(acts_full, columns, preferred_element_type=jnp.float32).astype(bf16)
    out_all, in_all = pl.pallas_call(
        gather_rotated_kernel,
        out_shape=(
            shaped(data_size, head_size, share, block),
            shaped(data_size, row_count, width),
        ),
        in_specs=[ANY] * 2,
        out_specs=(ANY,) * 2,
        scratch_shapes=[
            pltpu.VMEM((data_size, share, block), bf16),
            pltpu.VMEM((row_count, width), bf16),
        ]
        + sems(gather_copies, 8),
        compiler_params=talking(2),
        name="gather_rotated",
    )(rotated_out.reshape(data_size, share, block), rotated_in)
    out_all = out_all.reshape(data_size, row_count, block)

    seq_count = data_size * seq_here
    tile = min(width, 256)
    steps = width // tile
    corrections, scaled, tile_scores = pl.pallas_call(
        functools.partial(tile_kernel, seq_here, seq_len),
        grid=(steps,),
        out_shape=(
            shaped(block, width, dtype=jnp.float32),
            shaped(block, width),
            shaped(steps, seq_count, tile, dtype=jnp.float32),
        ),
        in_specs=[
            IN_SMEM,
            pl.BlockSpec((data_size, row_count, block), lambda i: (0, 0, 0)),
            pl.BlockSpec((data_size, row_count, tile), lambda i: (0, 0, i)),
        ],
        out_specs=(
            pl.BlockSpec((block, tile), lambda i: (0, i)),
            pl.BlockSpec((block, tile), lambda i: (0, i)),
            pl.BlockSpec((1, seq_count, tile), lambda i: (i, 0, 0)),
        ),
        scratch_shapes=[pltpu.VMEM((seq_count, block, tile), jnp.float32)],
        name="fit_tile",
    )(damping, out_all, in_all)

    partial_scores = jnp.broadcast_to(
        jnp.sum(tile_scores, axis=(0, 2))[:, None], (seq_count, 128)
    )
    piece = min(width, most_columns)
    turns = width // piece
    dma = pltpu.SemaphoreType.DMA
    update, score_sums = pl.pallas_call(
        finish_kernel,
        out_shape=(
            shaped(block, width),
            shaped(seq_count, 128, dtype=jnp.float32),
        ),
        in_specs=[IN_VMEM, ANY, ANY, IN_VMEM],
        out_specs=(IN_VMEM, IN_VMEM),
        scratch_shapes=[
            pltpu.VMEM((full_in, width), bf16),
            pltpu.VMEM((block, full_out), bf16),
            pltpu.VMEM((head_size, turns, block, piece), bf16),
            pltpu.VMEM((head_size, turns, block, piece), bf16),
            pltpu.VMEM((turns, data_size, block, piece), bf16),
            pltpu.VMEM((block, piece), jnp.float32),
            pltpu.VMEM((head_size, seq_count, 128), jnp.float32),
            pltpu.VMEM((data_size, seq_count, 128), jnp.float32),
            pltpu.VMEM((seq_count, 128), jnp.float32),
            dma((2, head_size, turns, halves)),
            dma((2, head_size, turns, halves)),
            dma((chips, turns, halves)),
            dma((chips, turns, halves)),
            dma((chips, turns, halves)),
            dma((chips, turns, halves)),
            dma((data_size + head_size,)),
            dma((data_size + head_size,)),
            dma((2,)),
        ],
        compiler_params=talking(3),
        name="finish",
    )(scaled, columns, basis_out, partial_scores)
    scores = score_sums[:, 0] / math.sqrt(full_in * full_out)
    return (update, corrections, scores)


def solution(mesh):
    in_specs = (
        P("dp", None, "head"),
        P("dp", None, "head"),
        P("dp", "head"),
        P("dp", "head"),
        P("dp", None),
        P("dp", None),
        P(),
    )
    out_specs = (P("dp", "head"), P("dp", "head"), P())
    return jax.shard_map(
        per_device, mesh=mesh, in_specs=in_specs, out_specs=out_specs, check_vma=False
    )
```
